32 devices in a mesh: pair: 2 (over core), shot: 16 (over z, y, x).
Axes of the slice: x: 2, y: 2, z: 4, core: 2. Of those that a mesh axis runs over, the one named last changes fastest.
Arguments:
- records: bfloat16 [4, 384, 384, 128], P('pair', 'shot'), may hold values from -6 to 6
- surface: float32 [16, 384], P('shot'), may hold values from 0.4 to 1.2
- mirror: int32 [4], replicated, may hold values from 0 to 3, as said below
Outputs:
- predicted: bfloat16 [4, 384, 384, 128], P('pair', 'shot')
The draws below stay inside these ranges and needn't reach their ends.
Inputs may be any that keep to these rules, and one draw needn't show every extreme that they name: mirror is an involution without fixed points: mirror[mirror[g]] = g and mirror[g] differs from g for every group.
All inputs are finite; a program needn't handle non-finite values.
Results may differ from the reference program's by a relative error of at most 0.0088.
Values may be sent and summed in bfloat16 or wider, within the bound.
A program may use at most 128 MiB of HBM per device.

```python
import math
import jax
import jax.numpy as jnp
from jax import lax

SHOTS = 384
RECV = 384
TIME = 128
FREQS = 16
ORDERS = 2
GROUPS = 4


def draw_mirror(key, part):
    order = jax.random.permutation(key, GROUPS).astype(jnp.int32)
    evens = order[0::2]
    odds = order[1::2]
    paired = jnp.zeros((GROUPS,), jnp.int32).at[evens].set(odds).at[odds].set(evens)
    return paired


def block_scale(key, extent, split, low, high):
    def one(dim, parts):
        heights = jax.random.uniform(jax.random.fold_in(jax.random.fold_in(key, 6), dim), (parts,), jnp.float32, low / len(split), high / len(split))
        return jnp.repeat(jnp.exp(heights), extent[dim] // parts).reshape((-1,) + (1,) * (len(extent) - dim - 1))

    gain = one(*split[0])
    for cut in split[1:]:
        gain = gain * one(*cut)
    return gain


def noise(stream_key, shape, width, reach, cuts=(), held_as=jnp.bfloat16):
    entries = jax.random.normal(stream_key, shape, jnp.float32) * width
    if len(cuts) > 0:
        entries = block_scale(stream_key, shape, cuts, -0.22, 0.18) * entries
    return jnp.clip(entries, min=-reach, max=reach).astype(held_as)


def setup_inputs(seed: int = 0) -> dict:
    streams_of = jax.random.split(jax.random.key(seed), 4)
    records = noise(streams_of[0], (GROUPS, SHOTS, RECV, TIME), 1.0, 6.0, ((0, 2), (1, 16)))
    surface = jnp.clip(jnp.exp(math.log(1.2) - 1.0986123 * jax.random.uniform(streams_of[1], (FREQS, RECV), jnp.float32) ** block_scale(streams_of[1], (FREQS, RECV), ((0, 16),), -0.2, 0.2)), 0.4, 1.2)
    mirror = draw_mirror(jax.random.fold_in(streams_of[3], 71), 0)
    return dict(records=records, surface=surface, mirror=mirror)


def make_tables(freqs, time):
    product = jnp.arange(1, freqs + 1, dtype=jnp.int32)[:, None] * jnp.arange(time, dtype=jnp.int32)[None, :] % time
    phase = product.astype(jnp.float32) * (2.0 * math.pi / time)
    cosine = jnp.cos(phase)
    sine = jnp.sin(phase)
    forward = (jnp.stack([cosine, -sine], axis=1) * math.sqrt(2.0 / time)).astype(jnp.bfloat16)
    inverse = (jnp.stack([cosine, -sine], axis=1) / math.sqrt(freqs)).astype(jnp.bfloat16)
    return (forward, inverse)

def real_dot(left, right):
    return jnp.dot(left.astype(jnp.float32), right.astype(jnp.float32), precision=lax.Precision.HIGHEST)

def one_frequency(items):
    own_spec, mate_spec, column_scale = items
    left = (own_spec.astype(jnp.float32) * column_scale[None, None, :]).astype(jnp.bfloat16)
    total = jnp.zeros(own_spec.shape, jnp.float32)
    for order_index in range(ORDERS):
        real_part = real_dot(left[0], mate_spec[0]) - real_dot(left[1], mate_spec[1])
        imag_part = real_dot(left[0], mate_spec[1]) + real_dot(left[1], mate_spec[0])
        product = jnp.stack([real_part, imag_part], axis=0)
        total = total + product
        if order_index + 1 < ORDERS:
            left = (product * column_scale[None, None, :]).astype(jnp.bfloat16)
    return total.astype(jnp.bfloat16)

def reference(records, surface, mirror):
    forward, inverse = make_tables(FREQS, TIME)

    def group_spectra(group_records):
        return jnp.einsum('kct,srt->kcsr', forward.astype(jnp.float32), group_records.astype(jnp.float32), precision=lax.Precision.HIGHEST).astype(jnp.bfloat16)
    spectra = lax.map(group_spectra, records)
    mates = spectra[mirror]
    scale = -surface.astype(jnp.float32) / math.sqrt(2.0 * RECV)

    def one_group(items):
        own_group, mate_group = items
        totals = lax.map(one_frequency, (own_group, mate_group, scale))
        predicted = jnp.einsum('kcsr,kct->srt', totals.astype(jnp.float32), inverse.astype(jnp.float32), precision=lax.Precision.HIGHEST)
        return predicted.astype(jnp.bfloat16)
    return lax.map(one_group, (spectra, mates))
```

```python
import functools
import math

import jax
import jax.numpy as jnp
from jax import lax
from jax.experimental import pallas as pl
from jax.experimental.pallas import tpu as pltpu
from jax.sharding import PartitionSpec as P

ORDERS = 2
MESH = pl.DeviceIdType.MESH


def make_tables(freqs, time):
    product = (
        jnp.arange(1, freqs + 1, dtype=jnp.int32)[:, None]
        * jnp.arange(time, dtype=jnp.int32)[None, :]
        % time
    )
    phase = product.astype(jnp.float32) * (2.0 * math.pi / time)
    cosine = jnp.cos(phase)
    sine = jnp.sin(phase)
    forward = (jnp.stack([cosine, -sine], axis=1) * math.sqrt(2.0 / time)).astype(jnp.bfloat16)
    inverse = (jnp.stack([cosine, -sine], axis=1) / math.sqrt(freqs)).astype(jnp.bfloat16)
    return (forward, inverse)


def kernel(
    chips, cores, target_ref, scale_ref, send_ref, out_ref,
    held, left, block, first, totals,
    own_sem, send_sems, recv_sems, pass_sems, pass_recv_sems, back_send_sems, back_recv_sems,
):
    me = lax.axis_index("shot")
    core = lax.axis_index("pair")
    groups, parts, shots, width = send_ref.shape[1:]
    freqs = parts // 2

    def chip(step):
        return lax.rem(me + step, chips)

    def back_chip(step):
        return lax.rem(me - step + chips, chips)

    def peer(step):
        return lax.rem(core + step, cores)

    def rows(index):
        return pl.ds(pl.multiple_of(index * shots, shots), shots)

    barrier = pltpu.get_barrier_semaphore()

    @pl.loop(1, chips)
    def _(step):
        pl.semaphore_signal(barrier, inc=1, device_id=(core, chip(step)), device_id_type=MESH)

    for step in range(1, cores):
        pl.semaphore_signal(barrier, inc=1, device_id=(peer(step), me), device_id_type=MESH)
    pl.semaphore_wait(barrier, chips + cores - 2)

    def spread(step):
        return pltpu.make_async_remote_copy(
            src_ref=send_ref.at[chip(step)],
            dst_ref=held.at[core, :, :, me],
            send_sem=send_sems.at[step],
            recv_sem=recv_sems.at[step],
            device_id=(core, chip(step)),
            device_id_type=MESH,
        )

    def hand_on(step, other):
        source = back_chip(step)
        return pltpu.make_async_remote_copy(
            src_ref=held.at[core, :, :, source],
            dst_ref=held.at[core, :, :, source],
            send_sem=pass_sems.at[other, step],
            recv_sem=pass_recv_sems.at[other, step],
            device_id=(peer(other), me),
            device_id_type=MESH,
        )

    @pl.loop(1, chips)
    def _(step):
        spread(step).start()

    own = pltpu.make_async_copy(send_ref.at[me], held.at[core, :, :, me], own_sem)
    own.start()
    own.wait()
    for other in range(1, cores):
        hand_on(0, other).start()

    @pl.loop(1, chips)
    def _(step):
        spread(step).wait_recv()
        for other in range(1, cores):
            hand_on(step, other).start()

    @pl.loop(0, chips)
    def _(step):
        for other in range(1, cores):
            hand_on(step, other).wait()

    def matrix(slot, group, part):
        value = held[slot, group, part].astype(jnp.float32)
        return value.reshape(chips * shots, width)

    def send_back(step, group):
        return pltpu.make_async_remote_copy(
            src_ref=totals.at[chip(step), group],
            dst_ref=out_ref.at[me, group],
            send_sem=back_send_sems.at[group, step],
            recv_sem=back_recv_sems.at[group, step],
            device_id=(core, chip(step)),
            device_id_type=MESH,
        )

    tall = chips * shots
    span = 16 if chips % 16 == 0 else chips
    tile = width if width % 256 == 0 else 2 * width
    for group in range(groups):
        mate = target_ref[group]
        mate_slot = mate // groups
        mate_group = lax.rem(mate, groups)
        for freq in range(freqs):
            scale = scale_ref[pl.ds(freq, 1), :]
            mate_re = matrix(mate_slot, mate_group, 2 * freq)
            mate_im = matrix(mate_slot, mate_group, 2 * freq + 1)
            block[:tall, :width] = mate_re.astype(jnp.bfloat16)
            block[tall:, width:] = mate_re.astype(jnp.bfloat16)
            block[:tall, width:] = mate_im.astype(jnp.bfloat16)
            block[tall:, :width] = (-mate_im).astype(jnp.bfloat16)
            for part in range(2):
                columns = slice(part * width, (part + 1) * width)
                value = matrix(core, group, 2 * freq + part)
                left[:, columns] = (value * scale).astype(jnp.bfloat16)
            for order in range(ORDERS):
                for top in range(0, chips, span):
                    band = slice(top * shots, (top + span) * shots)
                    pieces = []
                    for start in range(0, 2 * width, tile):
                        piece = jnp.dot(
                            left[band, :], block[:, start : start + tile],
                            preferred_element_type=jnp.float32,
                        )
                        if order > 0:
                            piece = piece + first[band, start : start + tile]
                        if order + 1 < ORDERS:
                            first[band, start : start + tile] = piece
                            pieces.append(piece)
                        else:
                            for low in range(start, start + tile, width):
                                total = piece[:, low - start : low - start + width]
                                totals[top : top + span, group, 2 * freq + low // width] = (
                                    total.reshape(span, shots, width).astype(jnp.bfloat16)
                                )
                    if order + 1 < ORDERS:
                        product = jnp.concatenate(pieces, axis=1) if len(pieces) > 1 else pieces[0]
                        wide = jnp.concatenate([scale, scale], axis=1)
                        left[band, :] = (product * wide).astype(jnp.bfloat16)

        @pl.loop(1, chips)
        def _(step):
            send_back(step, group).start()

        out_ref[me, group] = totals[me, group]

    @pl.loop(1, chips)
    def _(step):
        spread(step).wait_send()
        for group in range(groups):
            send_back(step, group).wait()


def local(records, surface, mirror):
    chips = lax.axis_size("shot")
    cores = lax.axis_size("pair")
    groups, shots, receivers, time = records.shape
    freqs = surface.shape[0]
    forward, inverse = make_tables(freqs * chips, time)
    spectra = jnp.einsum(
        "kct,gsrt->kgcsr", forward, records, preferred_element_type=jnp.float32
    ).astype(jnp.bfloat16)
    spectra = spectra.reshape(chips, freqs, groups, 2, shots, receivers)
    spectra = spectra.swapaxes(1, 2).reshape(chips, groups, 2 * freqs, shots, receivers)
    first_group = lax.axis_index("pair") * groups
    target = lax.dynamic_slice_in_dim(mirror, first_group, groups, 0)
    scale = -surface / math.sqrt(2.0 * receivers)
    tall = chips * shots
    block_shape = (chips, groups, 2 * freqs, shots, receivers)
    dma = pltpu.SemaphoreType.DMA
    total = pl.pallas_call(
        functools.partial(kernel, chips, cores),
        out_shape=jax.ShapeDtypeStruct(block_shape, jnp.bfloat16),
        in_specs=[
            pl.BlockSpec(memory_space=pltpu.SMEM),
            pl.BlockSpec(memory_space=pltpu.VMEM),
            pl.BlockSpec(memory_space=pltpu.VMEM),
        ],
        out_specs=pl.BlockSpec(memory_space=pltpu.VMEM),
        scratch_shapes=[
            pltpu.VMEM((cores, groups, 2 * freqs, chips, shots, receivers), jnp.bfloat16),
            pltpu.VMEM((tall, 2 * receivers), jnp.bfloat16),
            pltpu.VMEM((2 * tall, 2 * receivers), jnp.bfloat16),
            pltpu.VMEM((tall, 2 * receivers), jnp.float32),
            pltpu.VMEM(block_shape, jnp.bfloat16),
            dma,
            dma((chips,)),
            dma((chips,)),
            dma((cores, chips)),
            dma((cores, chips)),
            dma((groups, chips)),
            dma((groups, chips)),
        ],
        compiler_params=pltpu.CompilerParams(
            collective_id=0, has_side_effects=True, vmem_limit_bytes=60 * 1024 * 1024
        ),
    )(target, scale, spectra)
    total = total.reshape(chips, groups, freqs, 2, shots, receivers)
    table = inverse.reshape(chips, freqs, 2, time)
    return jnp.einsum(
        "ngfcsr,nfct->gsrt", total, table, preferred_element_type=jnp.float32
    ).astype(jnp.bfloat16)


def solution(mesh):
    return jax.shard_map(
        local,
        mesh=mesh,
        in_specs=(P("pair", "shot", None, None), P("shot", None), P()),
        out_specs=P("pair", "shot", None, None),
        check_vma=False,
    )
```

```python
import functools
import math

import jax
import jax.numpy as jnp
from jax import lax
from jax.experimental import pallas as pl
from jax.experimental.pallas import tpu as pltpu
from jax.sharding import PartitionSpec as P

ORDERS = 2
MESH = pl.DeviceIdType.MESH


def make_tables(freqs, time):
    product = (
        jnp.arange(1, freqs + 1, dtype=jnp.int32)[:, None]
        * jnp.arange(time, dtype=jnp.int32)[None, :]
        % time
    )
    phase = product.astype(jnp.float32) * (2.0 * math.pi / time)
    cosine = jnp.cos(phase)
    sine = jnp.sin(phase)
    forward = (jnp.stack([cosine, -sine], axis=1) * math.sqrt(2.0 / time)).astype(jnp.bfloat16)
    inverse = (jnp.stack([cosine, -sine], axis=1) / math.sqrt(freqs)).astype(jnp.bfloat16)
    return (forward, inverse)


def kernel(
    chips, cores, mirror_ref, surface_ref, forward_ref, records_ref, out_ref,
    traces, stage, send, held, left, block, first, totals, back,
    load_sems, own_sems, send_sems, recv_sems, pass_sems, pass_recv_sems, back_send_sems, back_recv_sems,
):
    me = lax.axis_index("shot")
    core = lax.axis_index("pair")
    groups, parts, shots, width = send.shape[1:]
    freqs = parts // 2
    loads = load_sems.shape[1]
    chunk = shots // loads

    def chip(step):
        return lax.rem(me + step, chips)

    def back_chip(step):
        return lax.rem(me - step + chips, chips)

    def peer(step):
        return lax.rem(core + step, cores)

    def far_first(index):
        turned = index + chips // 2 - 1
        return jnp.where(turned >= chips, turned - chips + 1, turned)

    def load(group, index):
        some = pl.ds(index * chunk, chunk)
        return pltpu.make_async_copy(
            records_ref.at[group, some], traces.at[group, some], load_sems.at[group, index]
        )

    for group in range(groups):
        for index in range(loads):
            load(group, index).start()

    barrier = pltpu.get_barrier_semaphore()

    @pl.loop(1, chips)
    def _(step):
        pl.semaphore_signal(barrier, inc=1, device_id=(core, chip(step)), device_id_type=MESH)

    for step in range(1, cores):
        pl.semaphore_signal(barrier, inc=1, device_id=(peer(step), me), device_id_type=MESH)

    def spread(step, group):
        return pltpu.make_async_remote_copy(
            src_ref=send.at[chip(step), group],
            dst_ref=held.at[core, group, :, me],
            send_sem=send_sems.at[group, step],
            recv_sem=recv_sems.at[group, step],
            device_id=(core, chip(step)),
            device_id_type=MESH,
        )

    def hand_on(step, other, group):
        source = back_chip(step)
        return pltpu.make_async_remote_copy(
            src_ref=held.at[core, group, :, source],
            dst_ref=held.at[core, group, :, source],
            send_sem=pass_sems.at[other, group, step],
            recv_sem=pass_recv_sems.at[other, group, step],
            device_id=(peer(other), me),
            device_id_type=MESH,
        )

    def keep(group):
        return pltpu.make_async_copy(
            send.at[me, group], held.at[core, group, :, me], own_sems.at[group]
        )

    def send_back(step, group):
        return pltpu.make_async_remote_copy(
            src_ref=totals.at[chip(step), group],
            dst_ref=back.at[me, group],
            send_sem=back_send_sems.at[group, step],
            recv_sem=back_recv_sems.at[group, step],
            device_id=(core, chip(step)),
            device_id_type=MESH,
        )

    for group in range(groups):
        for index in range(loads):
            load(group, index).wait()
            for shot in range(index * chunk, (index + 1) * chunk):
                stage[shot] = lax.dot_general(
                    forward_ref[...], traces[group, shot], (((1,), (1,)), ((), ())),
                    preferred_element_type=jnp.float32,
                )
        for row in range(chips * parts):
            send[row // parts, group, row % parts] = stage[:, row, :].astype(jnp.bfloat16)
        if group == 0:
            pl.semaphore_wait(barrier, chips + cores - 2)

        @pl.loop(1, chips)
        def _(index):
            spread(far_first(index), group).start()

        keep(group).start()

    for group in range(groups):
        keep(group).wait()
        for other in range(1, cores):
            hand_on(0, other, group).start()

        @pl.loop(1, chips)
        def _(index):
            step = far_first(index)
            spread(step, group).wait_recv()
            for other in range(1, cores):
                hand_on(step, other, group).start()

    @pl.loop(0, chips)
    def _(step):
        for group in range(groups):
            for other in range(1, cores):
                hand_on(step, other, group).wait()

    def matrix(slot, group, part):
        value = held[slot, group, part].astype(jnp.float32)
        return value.reshape(chips * shots, width)

    tall = chips * shots
    span = 16 if chips % 16 == 0 else chips
    tile = width if width % 256 == 0 else 2 * width
    for group in range(groups):
        mate = mirror_ref[core * groups + group]
        mate_slot = mate // groups
        mate_group = lax.rem(mate, groups)
        for freq in range(freqs):
            scale = -surface_ref[pl.ds(freq, 1), :] / math.sqrt(2.0 * width)
            mate_re = matrix(mate_slot, mate_group, 2 * freq)
            mate_im = matrix(mate_slot, mate_group, 2 * freq + 1)
            block[:tall, :width] = mate_re.astype(jnp.bfloat16)
            block[tall:, width:] = mate_re.astype(jnp.bfloat16)
            block[:tall, width:] = mate_im.astype(jnp.bfloat16)
            block[tall:, :width] = (-mate_im).astype(jnp.bfloat16)
            for part in range(2):
                columns = slice(part * width, (part + 1) * width)
                value = matrix(core, group, 2 * freq + part)
                left[:, columns] = (value * scale).astype(jnp.bfloat16)
            for order in range(ORDERS):
                for top in range(0, chips, span):
                    band = slice(top * shots, (top + span) * shots)
                    pieces = []
                    for start in range(0, 2 * width, tile):
                        piece = jnp.dot(
                            left[band, :], block[:, start : start + tile],
                            preferred_element_type=jnp.float32,
                        )
                        if order > 0:
                            piece = piece + first[band, start : start + tile]
                        if order + 1 < ORDERS:
                            first[band, start : start + tile] = piece
                            pieces.append(piece)
                        else:
                            for low in range(start, start + tile, width):
                                total = piece[:, low - start : low - start + width]
                                totals[top : top + span, group, 2 * freq + low // width] = (
                                    total.reshape(span, shots, width).astype(jnp.bfloat16)
                                )
                    if order + 1 < ORDERS:
                        product = jnp.concatenate(pieces, axis=1) if len(pieces) > 1 else pieces[0]
                        wide = jnp.concatenate([scale, scale], axis=1)
                        left[band, :] = (product * wide).astype(jnp.bfloat16)

        @pl.loop(1, chips)
        def _(index):
            send_back(far_first(index), group).start()

        back[me, group] = totals[me, group]

    @pl.loop(1, chips)
    def _(step):
        for group in range(groups):
            spread(step, group).wait_send()

    for group in range(groups):

        @pl.loop(1, chips)
        def _(index):
            send_back(far_first(index), group).wait()

        for row in range(chips * parts):
            stage[:, row, :] = back[row // parts, group, row % parts].astype(jnp.float32)
        out_ref[group] = stage[...].astype(jnp.bfloat16)


def local(records, surface, mirror):
    chips = lax.axis_size("shot")
    cores = lax.axis_size("pair")
    groups, shots, receivers, time = records.shape
    freqs = surface.shape[0]
    parts = 2 * freqs
    forward, inverse = make_tables(freqs * chips, time)
    tall = chips * shots
    loads = 4 if shots % 4 == 0 else 1
    block_shape = (chips, groups, parts, shots, receivers)
    dma = pltpu.SemaphoreType.DMA
    total = pl.pallas_call(
        functools.partial(kernel, chips, cores),
        out_shape=jax.ShapeDtypeStruct((groups, shots, chips * parts, receivers), jnp.bfloat16),
        in_specs=[
            pl.BlockSpec(memory_space=pltpu.SMEM),
            pl.BlockSpec(memory_space=pltpu.VMEM),
            pl.BlockSpec(memory_space=pltpu.VMEM),
            pl.BlockSpec(memory_space=pl.ANY),
        ],
        out_specs=pl.BlockSpec(memory_space=pltpu.VMEM),
        scratch_shapes=[
            pltpu.VMEM(records.shape, jnp.bfloat16),
            pltpu.VMEM((shots, chips * parts, receivers), jnp.float32),
            pltpu.VMEM(block_shape, jnp.bfloat16),
            pltpu.VMEM((cores, groups, parts, chips, shots, receivers), jnp.bfloat16),
            pltpu.VMEM((tall, 2 * receivers), jnp.bfloat16),
            pltpu.VMEM((2 * tall, 2 * receivers), jnp.bfloat16),
            pltpu.VMEM((tall, 2 * receivers), jnp.float32),
            pltpu.VMEM(block_shape, jnp.bfloat16),
            pltpu.VMEM(block_shape, jnp.bfloat16),
            dma((groups, loads)),
            dma((groups,)),
            dma((groups, chips)),
            dma((groups, chips)),
            dma((cores, groups, chips)),
            dma((cores, groups, chips)),
            dma((groups, chips)),
            dma((groups, chips)),
        ],
        compiler_params=pltpu.CompilerParams(
            collective_id=0, has_side_effects=True, vmem_limit_bytes=67043328
        ),
    )(mirror, surface, forward.reshape(chips * parts, time), records)
    return jnp.einsum(
        "gskr,kt->gsrt", total, inverse.reshape(chips * parts, time),
        preferred_element_type=jnp.float32,
    ).astype(jnp.bfloat16)


def solution(mesh):
    return jax.shard_map(
        local,
        mesh=mesh,
        in_specs=(P("pair", "shot", None, None), P("shot", None), P()),
        out_specs=P("pair", "shot", None, None),
        check_vma=False,
    )
```

```python
import functools
import math

import jax
import jax.numpy as jnp
from jax import lax
from jax.experimental import pallas as pl
from jax.experimental.pallas import tpu as pltpu
from jax.sharding import PartitionSpec as P

ORDERS = 2
MESH = pl.DeviceIdType.MESH


def make_tables(freqs, time):
    row = lax.broadcasted_iota(jnp.int32, (2 * freqs, time), 0)
    product = (row // 2 + 1) * lax.broadcasted_iota(jnp.int32, (2 * freqs, time), 1) % time
    phase = product.astype(jnp.float32) * (2.0 * math.pi / time)
    wave = jnp.where(row % 2 == 0, jnp.cos(phase), -jnp.sin(phase))
    forward = (wave * math.sqrt(2.0 / time)).astype(jnp.bfloat16)
    inverse = (wave / math.sqrt(freqs)).astype(jnp.bfloat16)
    return (forward, inverse)


def kernel(
    chips, cores, mirror_hbm, surface_hbm, forward_ref, records_ref, out_ref,
    traces, stage, send, held, left, block, first, totals, back, surface_ref, mirror_ref,
    small_sems, load_sems, own_sems, send_sems, recv_sems, pass_sems, pass_recv_sems,
    back_send_sems, back_recv_sems,
):
    me = lax.axis_index("shot")
    core = lax.axis_index("pair")
    groups, parts, shots, width = send.shape[1:]
    freqs = parts // 2
    loads = load_sems.shape[1]
    chunk = shots // loads
    half = chips // 2
    quarter = chips // 4
    across = jnp.where(me < half, 1, 0)

    def chip(step):
        return lax.rem(me + step, chips)

    def peer(step):
        return lax.rem(core + step, cores)

    def turned(index, size):
        inner = lax.rem(index + me, size) + size * (index // size)
        return lax.rem(across * size + inner, 2 * size)

    def middle(index):
        return quarter + turned(index, quarter)

    def outer(index):
        place = turned(index, quarter)
        return jnp.where(place < quarter, place, place + half)

    def load(group, index):
        some = pl.ds(index * chunk, chunk)
        return pltpu.make_async_copy(
            records_ref.at[group, some], traces.at[group, some], load_sems.at[group, index]
        )

    for group in range(groups):
        for index in range(loads):
            load(group, index).start()
    surface_copy = pltpu.make_async_copy(surface_hbm, surface_ref, small_sems.at[0])
    mirror_copy = pltpu.make_async_copy(mirror_hbm, mirror_ref, small_sems.at[1])
    surface_copy.start()
    mirror_copy.start()

    barrier = pltpu.get_barrier_semaphore()

    @pl.loop(1, chips)
    def _(step):
        pl.semaphore_signal(barrier, inc=1, device_id=(core, chip(step)), device_id_type=MESH)

    for step in range(1, cores):
        pl.semaphore_signal(barrier, inc=1, device_id=(peer(step), me), device_id_type=MESH)

    def spread(source, target, group):
        return pltpu.make_async_remote_copy(
            src_ref=send.at[target, group],
            dst_ref=held.at[core, group, :, source],
            send_sem=send_sems.at[group, target],
            recv_sem=recv_sems.at[group, source],
            device_id=(core, target),
            device_id_type=MESH,
        )

    def hand_on(source, other, group):
        return pltpu.make_async_remote_copy(
            src_ref=held.at[core, group, :, source],
            dst_ref=held.at[core, group, :, source],
            send_sem=pass_sems.at[other, group, source],
            recv_sem=pass_recv_sems.at[other, group, source],
            device_id=(peer(other), me),
            device_id_type=MESH,
        )

    def keep(group):
        return pltpu.make_async_copy(
            send.at[me, group], held.at[core, group, :, me], own_sems.at[group]
        )

    def send_back(source, target, group):
        return pltpu.make_async_remote_copy(
            src_ref=totals.at[target, group],
            dst_ref=back.at[source, group],
            send_sem=back_send_sems.at[group, target],
            recv_sem=back_recv_sems.at[group, source],
            device_id=(core, target),
            device_id_type=MESH,
        )

    def spread_half(target_of, group):
        @pl.loop(0, half)
        def _(index):
            target = target_of(index)

            @pl.when(target != me)
            def _():
                spread(me, target, group).start()

    for group in range(groups):
        for index in range(loads):
            load(group, index).wait()
            for shot in range(index * chunk, (index + 1) * chunk):
                stage[shot] = lax.dot_general(
                    forward_ref[...], traces[group, shot], (((1,), (1,)), ((), ())),
                    preferred_element_type=jnp.float32,
                )
        for row in range(chips * parts):
            send[row // parts, group, row % parts] = stage[:, row, :].astype(jnp.bfloat16)
        if group == 0:
            pl.semaphore_wait(barrier, chips + cores - 2)
        spread_half(middle, group)
        keep(group).start()
    for group in range(groups):
        spread_half(outer, group)

    surface_copy.wait()
    mirror_copy.wait()
    for group in range(groups):
        keep(group).wait()
        for other in range(1, cores):
            hand_on(me, other, group).start()

        @pl.loop(1, chips)
        def _(step):
            source = chip(step)
            spread(source, source, group).wait_recv()
            for other in range(1, cores):
                hand_on(source, other, group).start()

    @pl.loop(0, chips)
    def _(source):
        for group in range(groups):
            for other in range(1, cores):
                hand_on(source, other, group).wait()

    def matrix(slot, group, part):
        value = held[slot, group, part].astype(jnp.float32)
        return value.reshape(chips * shots, width)

    tall = chips * shots
    span = 16 if chips % 16 == 0 else chips
    tile = width if width % 256 == 0 else 2 * width
    for group in range(groups):
        mate = mirror_ref[core * groups + group]
        mate_slot = mate // groups
        mate_group = lax.rem(mate, groups)
        for freq in range(freqs):
            scale = -surface_ref[pl.ds(freq, 1), :] / math.sqrt(2.0 * width)
            mate_re = matrix(mate_slot, mate_group, 2 * freq)
            mate_im = matrix(mate_slot, mate_group, 2 * freq + 1)
            block[:tall, :width] = mate_re.astype(jnp.bfloat16)
            block[tall:, width:] = mate_re.astype(jnp.bfloat16)
            block[:tall, width:] = mate_im.astype(jnp.bfloat16)
            block[tall:, :width] = (-mate_im).astype(jnp.bfloat16)
            for part in range(2):
                columns = slice(part * width, (part + 1) * width)
                value = matrix(core, group, 2 * freq + part)
                left[:, columns] = (value * scale).astype(jnp.bfloat16)
            for order in range(ORDERS):
                for top in range(0, chips, span):
                    band = slice(top * shots, (top + span) * shots)
                    pieces = []
                    for start in range(0, 2 * width, tile):
                        piece = jnp.dot(
                            left[band, :], block[:, start : start + tile],
                            preferred_element_type=jnp.float32,
                        )
                        if order > 0:
                            piece = piece + first[band, start : start + tile]
                        if order + 1 < ORDERS:
                            first[band, start : start + tile] = piece
                            pieces.append(piece)
                        else:
                            for low in range(start, start + tile, width):
                                total = piece[:, low - start : low - start + width]
                                totals[top : top + span, group, 2 * freq + low // width] = (
                                    total.reshape(span, shots, width).astype(jnp.bfloat16)
                                )
                    if order + 1 < ORDERS:
                        product = jnp.concatenate(pieces, axis=1) if len(pieces) > 1 else pieces[0]
                        wide = jnp.concatenate([scale, scale], axis=1)
                        left[band, :] = (product * wide).astype(jnp.bfloat16)

        @pl.loop(0, chips)
        def _(index):
            target = turned(index, half)

            @pl.when(target != me)
            def _():
                send_back(me, target, group).start()

        for part in range(parts):
            own = totals[me, group, part].astype(jnp.float32)
            back[me, group, part] = own.astype(jnp.bfloat16)

    @pl.loop(1, chips)
    def _(step):
        for group in range(groups):
            spread(me, chip(step), group).wait_send()

    for group in range(groups):

        @pl.loop(0, chips)
        def _(source):
            @pl.when(source != me)
            def _():
                send_back(source, source, group).wait()

            for part in range(parts):
                value = back[source, group, part].astype(jnp.float32)
                stage[:, pl.ds(source * parts + part, 1), :] = value[:, None, :]

        out_ref[group] = stage[...].astype(jnp.bfloat16)


def local(records, surface, mirror):
    chips = lax.axis_size("shot")
    cores = lax.axis_size("pair")
    groups, shots, receivers, time = records.shape
    freqs = surface.shape[0]
    parts = 2 * freqs
    forward, inverse = make_tables(freqs * chips, time)
    tall = chips * shots
    loads = 4 if shots % 4 == 0 else 1
    block_shape = (chips, groups, parts, shots, receivers)
    dma = pltpu.SemaphoreType.DMA
    total_shape = (groups, shots, chips * parts, receivers)
    scratch = [
        (records.shape, jnp.bfloat16),
        ((shots, chips * parts, receivers), jnp.float32),
        (block_shape, jnp.bfloat16),
        ((cores, groups, parts, chips, shots, receivers), jnp.bfloat16),
        ((tall, 2 * receivers), jnp.bfloat16),
        ((2 * tall, 2 * receivers), jnp.bfloat16),
        ((tall, 2 * receivers), jnp.float32),
        (block_shape, jnp.bfloat16),
        (block_shape, jnp.bfloat16),
    ]
    held_bytes = sum(math.prod(shape) * jnp.dtype(kind).itemsize for shape, kind in scratch)
    roomy = held_bytes < 24 * 1024 * 1024
    grant = held_bytes + 8 * 1024 * 1024 if roomy else 67043328
    out_shape = pltpu.VMEM if roomy else jax.ShapeDtypeStruct
    total = pl.pallas_call(
        functools.partial(kernel, chips, cores),
        out_shape=out_shape(total_shape, jnp.bfloat16),
        in_specs=[
            pl.BlockSpec(memory_space=pltpu.HBM),
            pl.BlockSpec(memory_space=pltpu.HBM),
            pl.BlockSpec(memory_space=pltpu.VMEM),
            pl.BlockSpec(memory_space=pltpu.HBM),
        ],
        out_specs=pl.BlockSpec(memory_space=pltpu.VMEM),
        scratch_shapes=[
            *(pltpu.VMEM(shape, kind) for shape, kind in scratch),
            pltpu.VMEM(surface.shape, jnp.float32),
            pltpu.SMEM(mirror.shape, jnp.int32),
            dma((2,)),
            dma((groups, loads)),
            dma((groups,)),
            dma((groups, chips)),
            dma((groups, chips)),
            dma((cores, groups, chips)),
            dma((cores, groups, chips)),
            dma((groups, chips)),
            dma((groups, chips)),
        ],
        compiler_params=pltpu.CompilerParams(
            collective_id=0, has_side_effects=True, vmem_limit_bytes=grant
        ),
    )(
        pltpu.with_memory_space_constraint(mirror, pltpu.HBM),
        pltpu.with_memory_space_constraint(surface, pltpu.HBM),
        forward,
        pltpu.with_memory_space_constraint(records, pltpu.HBM),
    )
    return jnp.einsum("gskr,kt->gsrt", total, inverse, preferred_element_type=jnp.float32).astype(
        jnp.bfloat16
    )


def solution(mesh):
    return jax.shard_map(
        local,
        mesh=mesh,
        in_specs=(P("pair", "shot", None, None), P("shot", None), P()),
        out_specs=P("pair", "shot", None, None),
        check_vma=False,
    )
```

```python
import functools
import math

import jax
import jax.numpy as jnp
from jax import lax
from jax.experimental import pallas as pl
from jax.experimental.pallas import tpu as pltpu
from jax.sharding import PartitionSpec as P

ORDERS = 2
MESH = pl.DeviceIdType.MESH


def make_tables(freqs, time):
    row = lax.broadcasted_iota(jnp.int32, (2 * freqs, time), 0)
    product = (row // 2 + 1) * lax.broadcasted_iota(jnp.int32, (2 * freqs, time), 1) % time
    phase = product.astype(jnp.float32) * (2.0 * math.pi / time)
    wave = jnp.where(row % 2 == 0, jnp.cos(phase), -jnp.sin(phase))
    forward = (wave * math.sqrt(2.0 / time)).astype(jnp.bfloat16)
    inverse = (wave / math.sqrt(freqs)).astype(jnp.bfloat16)
    return (forward, inverse)


def kernel(
    chips, cores, mirror_hbm, surface_hbm, forward_ref, records_ref, out_ref,
    traces, stage, send, held, left, block, first, totals, back, surface_ref, mirror_ref,
    small_sems, load_sems, own_sems, send_sems, recv_sems, pass_sems, pass_recv_sems,
    back_send_sems, back_recv_sems,
):
    me = lax.axis_index("shot")
    core = lax.axis_index("pair")
    groups, parts, shots, width = send.shape[1:]
    freqs = parts // 2
    loads = load_sems.shape[1]
    chunk = shots // loads
    half = chips // 2
    quarter = chips // 4
    across = jnp.where(me < half, 0, 1)

    def chip(step):
        return lax.rem(me + step, chips)

    def peer(step):
        return lax.rem(core + step, cores)

    def turned(index, size):
        inner = lax.rem(index + me, size) + size * (index // size)
        return lax.rem(across * size + inner, 2 * size)

    def middle(index):
        return quarter + turned(index, quarter)

    def outer(index):
        place = turned(index, quarter)
        return jnp.where(place < quarter, place, place + half)

    def load(group, index):
        some = pl.ds(index * chunk, chunk)
        return pltpu.make_async_copy(
            records_ref.at[group, some], traces.at[group, some], load_sems.at[group, index]
        )

    for group in range(groups):
        for index in range(loads):
            load(group, index).start()
    surface_copy = pltpu.make_async_copy(surface_hbm, surface_ref, small_sems.at[0])
    mirror_copy = pltpu.make_async_copy(mirror_hbm, mirror_ref, small_sems.at[1])
    surface_copy.start()
    mirror_copy.start()

    barrier = pltpu.get_barrier_semaphore()

    @pl.loop(1, chips)
    def _(step):
        pl.semaphore_signal(barrier, inc=1, device_id=(core, chip(step)), device_id_type=MESH)

    for step in range(1, cores):
        pl.semaphore_signal(barrier, inc=1, device_id=(peer(step), me), device_id_type=MESH)

    def spread(source, target, group):
        return pltpu.make_async_remote_copy(
            src_ref=send.at[target, group],
            dst_ref=held.at[core, group, :, source],
            send_sem=send_sems.at[group, target],
            recv_sem=recv_sems.at[group, source],
            device_id=(core, target),
            device_id_type=MESH,
        )

    def hand_on(source, other, group):
        return pltpu.make_async_remote_copy(
            src_ref=held.at[core, group, :, source],
            dst_ref=held.at[core, group, :, source],
            send_sem=pass_sems.at[other, group, source],
            recv_sem=pass_recv_sems.at[other, group, source],
            device_id=(peer(other), me),
            device_id_type=MESH,
        )

    def keep(group):
        return pltpu.make_async_copy(
            send.at[me, group], held.at[core, group, :, me], own_sems.at[group]
        )

    def send_back(source, target, group):
        return pltpu.make_async_remote_copy(
            src_ref=totals.at[target, group],
            dst_ref=back.at[source, group],
            send_sem=back_send_sems.at[group, target],
            recv_sem=back_recv_sems.at[group, source],
            device_id=(core, target),
            device_id_type=MESH,
        )

    def spread_half(target_of, group):
        @pl.loop(0, half)
        def _(index):
            target = target_of(index)

            @pl.when(target != me)
            def _():
                spread(me, target, group).start()

    for group in range(groups):
        for index in range(loads):
            load(group, index).wait()
            for shot in range(index * chunk, (index + 1) * chunk):
                stage[shot] = lax.dot_general(
                    forward_ref[...], traces[group, shot], (((1,), (1,)), ((), ())),
                    preferred_element_type=jnp.float32,
                )
        for row in range(chips * parts):
            send[row // parts, group, row % parts] = stage[:, row, :].astype(jnp.bfloat16)
        if group == 0:
            pl.semaphore_wait(barrier, chips + cores - 2)
        spread_half(middle, group)
        keep(group).start()
    for group in range(groups):
        spread_half(outer, group)

    surface_copy.wait()
    mirror_copy.wait()
    for group in range(groups):
        keep(group).wait()
        for other in range(1, cores):
            hand_on(me, other, group).start()

        @pl.loop(1, chips)
        def _(step):
            source = chip(step)
            spread(source, source, group).wait_recv()
            for other in range(1, cores):
                hand_on(source, other, group).start()

    @pl.loop(0, chips)
    def _(source):
        for group in range(groups):
            for other in range(1, cores):
                hand_on(source, other, group).wait()

    def matrix(slot, group, part):
        value = held[slot, group, part].astype(jnp.float32)
        return value.reshape(chips * shots, width)

    tall = chips * shots
    span = 16 if chips % 16 == 0 else chips
    tile = width if width % 256 == 0 else 2 * width
    for group in range(groups):
        mate = mirror_ref[core * groups + group]
        mate_slot = mate // groups
        mate_group = lax.rem(mate, groups)
        for freq in range(freqs):
            scale = -surface_ref[pl.ds(freq, 1), :] / math.sqrt(2.0 * width)
            mate_re = matrix(mate_slot, mate_group, 2 * freq)
            mate_im = matrix(mate_slot, mate_group, 2 * freq + 1)
            block[:tall, :width] = mate_re.astype(jnp.bfloat16)
            block[tall:, width:] = mate_re.astype(jnp.bfloat16)
            block[:tall, width:] = mate_im.astype(jnp.bfloat16)
            block[tall:, :width] = (-mate_im).astype(jnp.bfloat16)
            for part in range(2):
                columns = slice(part * width, (part + 1) * width)
                value = matrix(core, group, 2 * freq + part)
                left[:, columns] = (value * scale).astype(jnp.bfloat16)
            for order in range(ORDERS):
                for top in range(0, chips, span):
                    band = slice(top * shots, (top + span) * shots)
                    pieces = []
                    for start in range(0, 2 * width, tile):
                        piece = jnp.dot(
                            left[band, :], block[:, start : start + tile],
                            preferred_element_type=jnp.float32,
                        )
                        if order > 0:
                            piece = piece + first[band, start : start + tile]
                        if order + 1 < ORDERS:
                            first[band, start : start + tile] = piece
                            pieces.append(piece)
                        else:
                            for low in range(start, start + tile, width):
                                total = piece[:, low - start : low - start + width]
                                totals[top : top + span, group, 2 * freq + low // width] = (
                                    total.reshape(span, shots, width).astype(jnp.bfloat16)
                                )
                    if order + 1 < ORDERS:
                        product = jnp.concatenate(pieces, axis=1) if len(pieces) > 1 else pieces[0]
                        wide = jnp.concatenate([scale, scale], axis=1)
                        left[band, :] = (product * wide).astype(jnp.bfloat16)

        @pl.loop(0, chips)
        def _(index):
            target = turned(index, half)

            @pl.when(target != me)
            def _():
                send_back(me, target, group).start()

        for part in range(parts):
            own = totals[me, group, part].astype(jnp.float32)
            back[me, group, part] = own.astype(jnp.bfloat16)

    @pl.loop(1, chips)
    def _(step):
        for group in range(groups):
            spread(me, chip(step), group).wait_send()

    for group in range(groups):

        @pl.loop(0, chips)
        def _(source):
            @pl.when(source != me)
            def _():
                send_back(source, source, group).wait()

            for part in range(parts):
                value = back[source, group, part].astype(jnp.float32)
                stage[:, pl.ds(source * parts + part, 1), :] = value[:, None, :]

        out_ref[group] = stage[...].astype(jnp.bfloat16)


def local(records, surface, mirror):
    chips = lax.axis_size("shot")
    cores = lax.axis_size("pair")
    groups, shots, receivers, time = records.shape
    freqs = surface.shape[0]
    parts = 2 * freqs
    forward, inverse = make_tables(freqs * chips, time)
    tall = chips * shots
    loads = 4 if shots % 4 == 0 else 1
    block_shape = (chips, groups, parts, shots, receivers)
    dma = pltpu.SemaphoreType.DMA
    total_shape = (groups, shots, chips * parts, receivers)
    scratch = [
        (records.shape, jnp.bfloat16),
        ((shots, chips * parts, receivers), jnp.float32),
        (block_shape, jnp.bfloat16),
        ((cores, groups, parts, chips, shots, receivers), jnp.bfloat16),
        ((tall, 2 * receivers), jnp.bfloat16),
        ((2 * tall, 2 * receivers), jnp.bfloat16),
        ((tall, 2 * receivers), jnp.float32),
        (block_shape, jnp.bfloat16),
        (block_shape, jnp.bfloat16),
    ]
    held_bytes = sum(math.prod(shape) * jnp.dtype(kind).itemsize for shape, kind in scratch)
    roomy = held_bytes < 24 * 1024 * 1024
    grant = held_bytes + 8 * 1024 * 1024 if roomy else 67043328
    out_shape = pltpu.VMEM if roomy else jax.ShapeDtypeStruct
    total = pl.pallas_call(
        functools.partial(kernel, chips, cores),
        out_shape=out_shape(total_shape, jnp.bfloat16),
        in_specs=[
            pl.BlockSpec(memory_space=pltpu.HBM),
            pl.BlockSpec(memory_space=pltpu.HBM),
            pl.BlockSpec(memory_space=pltpu.VMEM),
            pl.BlockSpec(memory_space=pltpu.HBM),
        ],
        out_specs=pl.BlockSpec(memory_space=pltpu.VMEM),
        scratch_shapes=[
            *(pltpu.VMEM(shape, kind) for shape, kind in scratch),
            pltpu.VMEM(surface.shape, jnp.float32),
            pltpu.SMEM(mirror.shape, jnp.int32),
            dma((2,)),
            dma((groups, loads)),
            dma((groups,)),
            dma((groups, chips)),
            dma((groups, chips)),
            dma((cores, groups, chips)),
            dma((cores, groups, chips)),
            dma((groups, chips)),
            dma((groups, chips)),
        ],
        compiler_params=pltpu.CompilerParams(
            collective_id=0, has_side_effects=True, vmem_limit_bytes=grant
        ),
    )(
        pltpu.with_memory_space_constraint(mirror, pltpu.HBM),
        pltpu.with_memory_space_constraint(surface, pltpu.HBM),
        forward,
        pltpu.with_memory_space_constraint(records, pltpu.HBM),
    )
    return jnp.einsum("gskr,kt->gsrt", total, inverse, preferred_element_type=jnp.float32).astype(
        jnp.bfloat16
    )


def solution(mesh):
    return jax.shard_map(
        local,
        mesh=mesh,
        in_specs=(P("pair", "shot", None, None), P("shot", None), P()),
        out_specs=P("pair", "shot", None, None),
        check_vma=False,
    )
```

```python
import functools
import math

import jax
import jax.numpy as jnp
from jax import lax
from jax.experimental import pallas as pl
from jax.experimental.pallas import tpu as pltpu
from jax.sharding import PartitionSpec as P

ORDERS = 2
MESH = pl.DeviceIdType.MESH


def make_tables(freqs, time):
    row = lax.broadcasted_iota(jnp.int32, (2 * freqs, time), 0)
    product = (row // 2 + 1) * lax.broadcasted_iota(jnp.int32, (2 * freqs, time), 1) % time
    phase = product.astype(jnp.float32) * (2.0 * math.pi / time)
    wave = jnp.where(row % 2 == 0, jnp.cos(phase), -jnp.sin(phase))
    forward = (wave * math.sqrt(2.0 / time)).astype(jnp.bfloat16)
    inverse = (wave / math.sqrt(freqs)).astype(jnp.bfloat16)
    return (forward, inverse)


def kernel(
    chips, cores, mirror_hbm, surface_hbm, forward_ref, records_ref, out_ref,
    traces, stage, send, held, left, block, first, totals, back, surface_ref, mirror_ref,
    small_sems, load_sems, own_sems, send_sems, recv_sems, pass_sems, pass_recv_sems,
    back_send_sems, back_recv_sems,
):
    me = lax.axis_index("shot")
    core = lax.axis_index("pair")
    groups, parts, shots, width = send.shape[1:]
    freqs = parts // 2
    loads = load_sems.shape[1]
    chunk = shots // loads
    half = chips // 2
    quarter = chips // 4
    across = jnp.where(me < half, 0, 1)

    def chip(step):
        return lax.rem(me + step, chips)

    def peer(step):
        return lax.rem(core + step, cores)

    def turned(index, size):
        inner = lax.rem(index + me, size) + size * (index // size)
        return lax.rem(across * size + inner, 2 * size)

    def middle(index):
        return quarter + turned(index, quarter)

    def outer(index):
        place = turned(index, quarter)
        return jnp.where(place < quarter, place, place + half)

    def load(group, index):
        some = pl.ds(index * chunk, chunk)
        return pltpu.make_async_copy(
            records_ref.at[group, some], traces.at[group, some], load_sems.at[group, index]
        )

    for group in range(groups):
        for index in range(loads):
            load(group, index).start()
    surface_copy = pltpu.make_async_copy(surface_hbm, surface_ref, small_sems.at[0])
    mirror_copy = pltpu.make_async_copy(mirror_hbm, mirror_ref, small_sems.at[1])
    surface_copy.start()
    mirror_copy.start()

    barrier = pltpu.get_barrier_semaphore()

    @pl.loop(1, chips)
    def _(step):
        pl.semaphore_signal(barrier, inc=1, device_id=(core, chip(step)), device_id_type=MESH)

    for step in range(1, cores):
        pl.semaphore_signal(barrier, inc=1, device_id=(peer(step), me), device_id_type=MESH)

    def spread(source, target, group):
        return pltpu.make_async_remote_copy(
            src_ref=send.at[target, group],
            dst_ref=held.at[core, group, :, source],
            send_sem=send_sems.at[group, target],
            recv_sem=recv_sems.at[group, source],
            device_id=(core, target),
            device_id_type=MESH,
        )

    def hand_on(source, other, group):
        return pltpu.make_async_remote_copy(
            src_ref=held.at[core, group, :, source],
            dst_ref=held.at[core, group, :, source],
            send_sem=pass_sems.at[other, group, source],
            recv_sem=pass_recv_sems.at[other, group, source],
            device_id=(peer(other), me),
            device_id_type=MESH,
        )

    def keep(group):
        return pltpu.make_async_copy(
            send.at[me, group], held.at[core, group, :, me], own_sems.at[group]
        )

    def send_back(source, target, group):
        return pltpu.make_async_remote_copy(
            src_ref=totals.at[target, group],
            dst_ref=back.at[source, group],
            send_sem=back_send_sems.at[group, target],
            recv_sem=back_recv_sems.at[group, source],
            device_id=(core, target),
            device_id_type=MESH,
        )

    def spread_half(target_of, group):
        @pl.loop(0, half)
        def _(index):
            target = target_of(index)

            @pl.when(target != me)
            def _():
                spread(me, target, group).start()

    for group in range(groups):
        for index in range(loads):
            load(group, index).wait()
            for shot in range(index * chunk, (index + 1) * chunk):
                stage[shot] = lax.dot_general(
                    forward_ref[...], traces[group, shot], (((1,), (1,)), ((), ())),
                    preferred_element_type=jnp.float32,
                )
        for row in range(chips * parts):
            send[row // parts, group, row % parts] = stage[:, row, :].astype(jnp.bfloat16)
        if group == 0:
            pl.semaphore_wait(barrier, chips + cores - 2)
        spread_half(middle, group)
        keep(group).start()
    for group in range(groups):
        spread_half(outer, group)

    surface_copy.wait()
    mirror_copy.wait()
    for group in range(groups):
        keep(group).wait()
        for other in range(1, cores):
            hand_on(me, other, group).start()

        @pl.loop(0, chips)
        def _(index):
            source = turned(index, half)

            @pl.when(source != me)
            def _():
                spread(source, source, group).wait_recv()
                for other in range(1, cores):
                    hand_on(source, other, group).start()

    @pl.loop(0, chips)
    def _(source):
        for group in range(groups):
            for other in range(1, cores):
                hand_on(source, other, group).wait()

    def matrix(slot, group, part):
        value = held[slot, group, part].astype(jnp.float32)
        return value.reshape(chips * shots, width)

    tall = chips * shots
    span = 16 if chips % 16 == 0 else chips
    tile = width if width % 256 == 0 else 2 * width
    for group in range(groups):
        mate = mirror_ref[core * groups + group]
        mate_slot = mate // groups
        mate_group = lax.rem(mate, groups)
        for freq in range(freqs):
            scale = -surface_ref[pl.ds(freq, 1), :] / math.sqrt(2.0 * width)
            mate_re = matrix(mate_slot, mate_group, 2 * freq)
            mate_im = matrix(mate_slot, mate_group, 2 * freq + 1)
            block[:tall, :width] = mate_re.astype(jnp.bfloat16)
            block[tall:, width:] = mate_re.astype(jnp.bfloat16)
            block[:tall, width:] = mate_im.astype(jnp.bfloat16)
            block[tall:, :width] = (-mate_im).astype(jnp.bfloat16)
            for part in range(2):
                columns = slice(part * width, (part + 1) * width)
                value = matrix(core, group, 2 * freq + part)
                left[:, columns] = (value * scale).astype(jnp.bfloat16)
            for order in range(ORDERS):
                for top in range(0, chips, span):
                    band = slice(top * shots, (top + span) * shots)
                    pieces = []
                    for start in range(0, 2 * width, tile):
                        piece = jnp.dot(
                            left[band, :], block[:, start : start + tile],
                            preferred_element_type=jnp.float32,
                        )
                        if order > 0:
                            piece = piece + first[band, start : start + tile]
                        if order + 1 < ORDERS:
                            first[band, start : start + tile] = piece
                            pieces.append(piece)
                        else:
                            for low in range(start, start + tile, width):
                                total = piece[:, low - start : low - start + width]
                                totals[top : top + span, group, 2 * freq + low // width] = (
                                    total.reshape(span, shots, width).astype(jnp.bfloat16)
                                )
                    if order + 1 < ORDERS:
                        product = jnp.concatenate(pieces, axis=1) if len(pieces) > 1 else pieces[0]
                        wide = jnp.concatenate([scale, scale], axis=1)
                        left[band, :] = (product * wide).astype(jnp.bfloat16)

        @pl.loop(0, chips)
        def _(index):
            target = turned(index, half)

            @pl.when(target != me)
            def _():
                send_back(me, target, group).start()

        for part in range(parts):
            own = totals[me, group, part].astype(jnp.float32)
            back[me, group, part] = own.astype(jnp.bfloat16)

    @pl.loop(1, chips)
    def _(step):
        for group in range(groups):
            spread(me, chip(step), group).wait_send()

    for group in range(groups):

        @pl.loop(0, chips)
        def _(index):
            source = turned(index, half)

            @pl.when(source != me)
            def _():
                send_back(source, source, group).wait()

            for part in range(parts):
                value = back[source, group, part].astype(jnp.float32)
                stage[:, pl.ds(source * parts + part, 1), :] = value[:, None, :]

        out_ref[group] = stage[...].astype(jnp.bfloat16)


def local(records, surface, mirror):
    chips = lax.axis_size("shot")
    cores = lax.axis_size("pair")
    groups, shots, receivers, time = records.shape
    freqs = surface.shape[0]
    parts = 2 * freqs
    forward, inverse = make_tables(freqs * chips, time)
    tall = chips * shots
    loads = 4 if shots % 4 == 0 else 1
    block_shape = (chips, groups, parts, shots, receivers)
    dma = pltpu.SemaphoreType.DMA
    total_shape = (groups, shots, chips * parts, receivers)
    scratch = [
        (records.shape, jnp.bfloat16),
        ((shots, chips * parts, receivers), jnp.float32),
        (block_shape, jnp.bfloat16),
        ((cores, groups, parts, chips, shots, receivers), jnp.bfloat16),
        ((tall, 2 * receivers), jnp.bfloat16),
        ((2 * tall, 2 * receivers), jnp.bfloat16),
        ((tall, 2 * receivers), jnp.float32),
        (block_shape, jnp.bfloat16),
        (block_shape, jnp.bfloat16),
    ]
    held_bytes = sum(math.prod(shape) * jnp.dtype(kind).itemsize for shape, kind in scratch)
    roomy = held_bytes < 24 * 1024 * 1024
    grant = held_bytes + 8 * 1024 * 1024 if roomy else 67043328
    out_shape = pltpu.VMEM if roomy else jax.ShapeDtypeStruct
    total = pl.pallas_call(
        functools.partial(kernel, chips, cores),
        out_shape=out_shape(total_shape, jnp.bfloat16),
        in_specs=[
            pl.BlockSpec(memory_space=pltpu.HBM),
            pl.BlockSpec(memory_space=pltpu.HBM),
            pl.BlockSpec(memory_space=pltpu.VMEM),
            pl.BlockSpec(memory_space=pltpu.HBM),
        ],
        out_specs=pl.BlockSpec(memory_space=pltpu.VMEM),
        scratch_shapes=[
            *(pltpu.VMEM(shape, kind) for shape, kind in scratch),
            pltpu.VMEM(surface.shape, jnp.float32),
            pltpu.SMEM(mirror.shape, jnp.int32),
            dma((2,)),
            dma((groups, loads)),
            dma((groups,)),
            dma((groups, chips)),
            dma((groups, chips)),
            dma((cores, groups, chips)),
            dma((cores, groups, chips)),
            dma((groups, chips)),
            dma((groups, chips)),
        ],
        compiler_params=pltpu.CompilerParams(
            collective_id=0, has_side_effects=True, vmem_limit_bytes=grant
        ),
    )(
        pltpu.with_memory_space_constraint(mirror, pltpu.HBM),
        pltpu.with_memory_space_constraint(surface, pltpu.HBM),
        forward,
        pltpu.with_memory_space_constraint(records, pltpu.HBM),
    )
    return jnp.einsum("gskr,kt->gsrt", total, inverse, preferred_element_type=jnp.float32).astype(
        jnp.bfloat16
    )


def solution(mesh):
    return jax.shard_map(
        local,
        mesh=mesh,
        in_specs=(P("pair", "shot", None, None), P("shot", None), P()),
        out_specs=P("pair", "shot", None, None),
        check_vma=False,
    )
```
